32 devices in a mesh: grp: 4 (over x, core), blk: 8 (over z, y).
Axes of the slice: x: 2, y: 2, z: 4, core: 2. Of those that a mesh axis runs over, the one named last changes fastest.
Arguments:
- masses: bfloat16 [8, 2, 256, 256], P('blk'), may hold values from -3 to 3
- spins: int32 [8, 256], P('blk'), may hold values from 0 to 1
- shift_table: int32 [32, 256], P('blk'), may hold values from 0 to 255, as said below
- flip_table: int32 [32, 256], P('blk'), may hold values from 0 to 255, as said below
- ph_in: float32 [2, 32, 256, 256], P(None, 'blk', 'grp'), may hold values from -6 to 6
- pp_in: float32 [2, 32, 256, 256], P(None, 'blk', 'grp'), may hold values from -6 to 6
Outputs:
- ph_out: float32 [2, 32, 256, 256], P(None, 'blk', 'grp')
- pp_out: float32 [2, 32, 256, 256], P(None, 'blk', 'grp')
The draws below stay inside these ranges and needn't reach their ends.
Inputs may be any that keep to these rules, and one draw needn't show every extreme that they name: Row t of shift_table maps w * 16 + k to ((w + n_t) mod 16) * 16 + (k + q_t) mod 16 for some integers n_t, q_t of the transfer; every row is a permutation. Row t of flip_table maps w * 16 + k to ((n_t - w - 1) mod 16) * 16 + (q_t - k) mod 16 with the same n_t, q_t as shift_table's row t.
All inputs are finite; a program needn't handle non-finite values.
Results may differ from the reference program's by a relative error of at most 0.0064.
Values may be sent and summed in bfloat16 or wider, within the bound.
A program may use at most 128 MiB of HBM per device.

```python
import math
import jax
import jax.numpy as jnp
from jax import lax

NW = 16
NK = 16
ORDER = 256
WALK_DEV = 1
TR_DEV = 4
WALKERS = 8
TRANS = 32
SHIFTS = 7
N_BLK = 8


def table_moves(key):
    momentum_move = jax.random.randint(jax.random.fold_in(key, 71), (TRANS,), 0, NK)
    frequency_move = jax.random.randint(jax.random.fold_in(key, 72), (TRANS,), 0, NW)
    return (momentum_move, frequency_move)


def draw_shift_table(key, part):
    momentum_move, frequency_move = table_moves(key)
    index = jnp.arange(NW * NK, dtype=jnp.int32)
    frequency = index // NK
    momentum = index % NK
    result = (frequency[None, :] + frequency_move[:, None]) % NW * NK + (momentum[None, :] + momentum_move[:, None]) % NK
    return result.astype(jnp.int32)


def draw_flip_table(key, part):
    momentum_move, frequency_move = table_moves(key)
    index = jnp.arange(NW * NK, dtype=jnp.int32)
    frequency = index // NK
    momentum = index % NK
    result = (frequency_move[:, None] - frequency[None, :] - 1) % NW * NK + (momentum_move[:, None] - momentum[None, :]) % NK
    return result.astype(jnp.int32)


def plant(values, own_key, smallest, top_value):
    extent = values.shape
    spot = [jax.random.randint(jax.random.fold_in(own_key, axis), (), 0, extent[axis]) for axis in range(len(extent))]
    values = values.at[tuple(spot)].set(smallest)
    longest = extent.index(max(extent))
    spot[longest] = (spot[longest] + 1) % extent[longest]
    return values.at[tuple(spot)].set(top_value)


def steps_of(key, shape, cuts, least, largest):
    level, own = 1.0, jax.random.fold_in(key, 6)
    for position, blocks in cuts:
        draws = jnp.exp(jax.random.uniform(jax.random.fold_in(own, position), (blocks,), jnp.float32, least / len(cuts), largest / len(cuts)))
        level = level * jnp.repeat(draws, shape[position] // blocks).reshape([-1 if axis == position else 1 for axis in range(len(shape))])
    return level


def noise(rng, extent, width, bound, cuts=(), kind=jnp.bfloat16):
    array = width * jax.random.normal(rng, extent, jnp.float32)
    if cuts:
        array = array * steps_of(rng, extent, cuts, -0.22, 0.18)
    return jnp.clip(array, -bound, bound).astype(kind)


def setup_inputs(seed: int = 0) -> dict:
    key_of = jax.random.split(jax.random.key(seed), 7)
    return {
        "masses": noise(key_of[0], (WALKERS, 2, ORDER, ORDER), 0.5, 3.0, ((0, 8),)),
        "spins": plant(jax.random.randint(key_of[1], (WALKERS, ORDER), 0, 2), jax.random.fold_in(key_of[1], 1), 0, 1).astype(jnp.int32),
        "shift_table": draw_shift_table(jax.random.fold_in(key_of[6], 71), 0),
        "flip_table": draw_flip_table(jax.random.fold_in(key_of[6], 71), 0),
        "ph_in": noise(key_of[4], (2, TRANS, ORDER, ORDER), 1.0, 6.0, ((1, 8), (2, 4)), jnp.float32),
        "pp_in": noise(key_of[5], (2, TRANS, ORDER, ORDER), 1.0, 6.0, ((1, 8), (2, 4)), jnp.float32),
    }


COUPLING = 0.5

def dft_tables():
    index = jnp.arange(NW * NK, dtype=jnp.int32)
    frequency = index // NK
    momentum = index % NK
    numerator = ((2 * frequency[:, None] + 1) * frequency[None, :] * NK - 2 * momentum[:, None] * momentum[None, :] * NW) % (2 * NW * NK)
    phase = numerator.astype(jnp.float32) * (math.pi / (NW * NK))
    norm_scale = 1.0 / math.sqrt(NW * NK)
    return ((jnp.cos(phase) * norm_scale).astype(jnp.bfloat16), (jnp.sin(phase) * norm_scale).astype(jnp.bfloat16))

def build(masses, spins, real_table, imag_table):
    signed = (2 * spins - 1).astype(jnp.float32)
    factors = jnp.stack([jnp.exp(COUPLING * signed), jnp.exp(-COUPLING * signed)], 1)
    scaled = (masses.astype(jnp.float32) * factors[:, :, None, :]).astype(jnp.bfloat16).astype(jnp.float32)
    first_real = jnp.einsum('ri,wsij->wsrj', real_table.astype(jnp.float32), scaled).astype(jnp.bfloat16)
    first_imag = jnp.einsum('ri,wsij->wsrj', imag_table.astype(jnp.float32), scaled).astype(jnp.bfloat16)
    joined = jnp.concatenate([first_real, first_imag], -1).astype(jnp.float32)
    big_table = jnp.concatenate([jnp.concatenate([real_table.T, -imag_table.T], 1), jnp.concatenate([imag_table.T, real_table.T], 1)], 0).astype(jnp.float32)
    second = jnp.einsum('wsri,ij->wsrj', joined, big_table)
    order = real_table.shape[1]
    return jnp.stack([second[..., :order], second[..., order:]], 2).astype(jnp.bfloat16)

def reference(masses, spins, shift_table, flip_table, ph_in, pp_in):
    real_table, imag_table = dft_tables()
    propagator = build(masses, spins, real_table, imag_table)

    def one_block(block, totals):
        ph_total, pp_total = totals
        homes = (block - jnp.arange(SHIFTS + 1, dtype=jnp.int32)) % N_BLK
        walker_ids = (homes[:, None] * WALK_DEV + jnp.arange(WALK_DEV, dtype=jnp.int32)[None, :]).reshape(-1)
        props = propagator[walker_ids].astype(jnp.float32)
        begin = (block * TR_DEV).astype(jnp.int32)
        shifts = lax.dynamic_slice_in_dim(shift_table, begin, TR_DEV, 0)
        flips = lax.dynamic_slice_in_dim(flip_table, begin, TR_DEV, 0)
        mirrored = jnp.swapaxes(props, 3, 4)[:, :, :, None]
        moved = props[:, :, :, shifts[:, :, None], shifts[:, None, :]]
        ph_real = lax.optimization_barrier(jnp.sum(mirrored[:, :, 0] * moved[:, :, 0] - mirrored[:, :, 1] * moved[:, :, 1], axis=(0, 1)))
        ph_imag = lax.optimization_barrier(jnp.sum(mirrored[:, :, 0] * moved[:, :, 1] + mirrored[:, :, 1] * moved[:, :, 0], axis=(0, 1)))
        upper = props[:, 0][:, :, None]
        lowered = props[:, 1][:, :, flips[:, :, None], flips[:, None, :]]
        pp_real = lax.optimization_barrier(jnp.sum(upper[:, 0] * lowered[:, 0] - upper[:, 1] * lowered[:, 1], axis=0))
        pp_imag = lax.optimization_barrier(jnp.sum(upper[:, 0] * lowered[:, 1] + upper[:, 1] * lowered[:, 0], axis=0))
        ph_old = lax.dynamic_slice_in_dim(ph_total, begin, TR_DEV, 1)
        pp_old = lax.dynamic_slice_in_dim(pp_total, begin, TR_DEV, 1)
        ph_total = lax.dynamic_update_slice_in_dim(ph_total, ph_old + jnp.stack([ph_real, ph_imag]), begin, 1)
        pp_total = lax.dynamic_update_slice_in_dim(pp_total, pp_old + jnp.stack([pp_real, pp_imag]), begin, 1)
        return (ph_total, pp_total)
    ph_out, pp_out = lax.fori_loop(0, N_BLK, one_block, (ph_in, pp_in))
    return (ph_out, pp_out)
```

```python
import functools
import math

import jax
import jax.numpy as jnp
from jax import lax
from jax.experimental import pallas as pl
from jax.experimental.pallas import tpu as pltpu
from jax.sharding import PartitionSpec as P

NW = 16
NK = 16
COUPLING = 0.5
MESH = pl.DeviceIdType.MESH
NT = (((1,), (1,)), ((), ()))


def angle(steps):
    return steps.astype(jnp.float32) * (math.pi / NW)


def base_steps(row, col):
    return ((2 * (row // NK) + 1) * (col // NK) - 2 * (row % NK) * (col % NK)) % (2 * NW)


def move_steps(freq, mom, col):
    return (2 * freq * (col // NK) - 2 * mom * (col % NK)) % (2 * NW)


def kernel(
    blocks, groups, reach, shift_ref, masses_ref, spins_ref, ph_ref, pp_ref, ph_out, pp_out,
    held, held_spins, col_table, sh_cols, fl_cols, band, sh_rows, fl_rows,
    x_ph, x_pp, fixed, recv_sem, spin_recv, direct_sem, spin_send, core_sem, far_sem, relay_sem,
    local_sem,
):
    group = lax.axis_index("grp")
    block = lax.axis_index("blk")
    order = held.shape[-1]
    walkers = held.shape[1]
    trans = ph_out.shape[1]
    height = order // groups
    chips = groups // 2
    chip, core = group // 2, group % 2
    partner = chip * 2 + (1 - core)
    f32, bf16 = jnp.float32, jnp.bfloat16

    def far(step):
        return lax.rem(chip + step, chips) * 2 + core

    def rows_of(piece):
        return pl.ds(pl.multiple_of(piece * height, height), height)

    barrier = pltpu.get_barrier_semaphore()
    for offset in range(1, reach + 1):
        source = lax.rem(block - offset + blocks, blocks)
        pl.semaphore_signal(barrier, inc=1, device_id=(group, source), device_id_type=MESH)
    pl.semaphore_signal(barrier, inc=1, device_id=(partner, block), device_id_type=MESH)
    for step in range(1, chips):
        pl.semaphore_signal(barrier, inc=1, device_id=(far(step), block), device_id_type=MESH)

    local = [
        pltpu.make_async_copy(masses_ref, held.at[0], local_sem.at[0]),
        pltpu.make_async_copy(spins_ref, held_spins.at[0], local_sem.at[1]),
        pltpu.make_async_copy(ph_ref, ph_out, local_sem.at[2]),
        pltpu.make_async_copy(pp_ref, pp_out, local_sem.at[3]),
    ]
    for copy in local:
        copy.start()
    pl.semaphore_wait(barrier, reach + chips)

    def direct(offset):
        target = (group, lax.rem(block + offset, blocks))
        return (
            pltpu.make_async_remote_copy(
                src_ref=masses_ref.at[:, :, rows_of(group)],
                dst_ref=held.at[offset, :, :, rows_of(group)],
                send_sem=direct_sem.at[offset],
                recv_sem=recv_sem.at[offset, group],
                device_id=target,
                device_id_type=MESH,
            ),
            pltpu.make_async_remote_copy(
                src_ref=spins_ref,
                dst_ref=held_spins.at[offset],
                send_sem=spin_send.at[offset],
                recv_sem=spin_recv.at[offset],
                device_id=target,
                device_id_type=MESH,
            ),
        )

    def passed(offset, piece, target, send_sem):
        view = held.at[offset, :, :, rows_of(piece)]
        return pltpu.make_async_remote_copy(
            src_ref=view,
            dst_ref=view,
            send_sem=send_sem,
            recv_sem=recv_sem.at[offset, piece],
            device_id=(target, block),
            device_id_type=MESH,
        )

    def to_core(offset):
        return passed(offset, group, partner, core_sem.at[offset])

    def to_far(offset, step):
        return passed(offset, group, far(step), far_sem.at[step, offset])

    def relay(offset, step):
        return passed(offset, far(step), partner, relay_sem.at[step, offset])

    def arrival(offset, piece):
        return passed(offset, piece, partner, core_sem.at[offset])

    for offset in range(1, reach + 1):
        for copy in direct(offset):
            copy.start()

    norm = 1.0 / math.sqrt(NW * NK)
    index_col = lax.broadcasted_iota(jnp.int32, (order, 128), 0)
    lane = lax.broadcasted_iota(jnp.int32, (order, 128), 1)
    freq = jnp.zeros((order, 128), jnp.int32)
    mom = jnp.zeros((order, 128), jnp.int32)
    for t in range(trans):
        start = shift_ref[t, 0]
        freq = jnp.where(lane == t, start // NK, freq)
        mom = jnp.where(lane == t, start % NK, mom)
    move = angle(move_steps(freq, mom, index_col))
    move_cos, move_sin = jnp.cos(move), jnp.sin(move)

    def put_cols(ref, t, real, imag):
        where = (slice(None),) if t is None else (t, slice(None))
        real, imag = (real * norm).astype(bf16), (imag * norm).astype(bf16)
        ref[where[:-1] + (slice(0, order), slice(0, order))] = real
        ref[where[:-1] + (slice(0, order), slice(order, 2 * order))] = -imag
        ref[where[:-1] + (slice(order, 2 * order), slice(0, order))] = imag
        ref[where[:-1] + (slice(order, 2 * order), slice(order, 2 * order))] = real

    site = lax.broadcasted_iota(jnp.int32, (order, order), 0)
    momentum = lax.broadcasted_iota(jnp.int32, (order, order), 1)
    phase = angle(base_steps(momentum, site))
    cos, sin = jnp.cos(phase), jnp.sin(phase)
    put_cols(col_table, None, cos, sin)
    for t in range(trans):
        mc, ms = move_cos[:, t : t + 1], move_sin[:, t : t + 1]
        cc, ss, sc, cs = mc * cos, ms * sin, ms * cos, mc * sin
        put_cols(sh_cols, t, cc - ss, sc + cs)
        put_cols(fl_cols, t, cc + ss, sc - cs)

    row = lax.broadcasted_iota(jnp.int32, (height, order), 0) + group * height
    column = lax.broadcasted_iota(jnp.int32, (height, order), 1)
    phase = angle(base_steps(row, column))
    cos, sin = jnp.cos(phase), jnp.sin(phase)
    band[0:height, :] = (cos * norm).astype(bf16)
    band[height : 2 * height, :] = (sin * norm).astype(bf16)
    col8 = lax.broadcasted_iota(jnp.int32, (8, order), 1)
    for t in range(trans):
        start = shift_ref[t, 0]
        move = angle(move_steps(start // NK, start % NK, col8))
        mc, ms = jnp.cos(move)[0:1], jnp.sin(move)[0:1]
        cc, ss, sc, cs = mc * cos, ms * sin, ms * cos, mc * sin
        first = 2 * t * height
        sh_rows[first : first + height, :] = ((cc - ss) * norm).astype(bf16)
        sh_rows[first + height : first + 2 * height, :] = ((sc + cs) * norm).astype(bf16)
        fl_rows[first : first + height, :] = ((cc + ss) * norm).astype(bf16)
        fl_rows[first + height : first + 2 * height, :] = ((sc - cs) * norm).astype(bf16)

    def dot(a, b):
        return jnp.dot(a, b, preferred_element_type=f32)

    def absorb(slot):
        for w in range(walkers):
            place = pl.ds(pl.multiple_of((slot * walkers + w) * height, height), height)
            signed = (2 * held_spins[slot, w : w + 1, :] - 1).astype(f32)
            lefts = []
            for s in range(2):
                factor = jnp.exp((COUPLING if s == 0 else -COUPLING) * signed)
                scaled = (held[slot, w, s].astype(f32) * factor).astype(bf16)
                moved = dot(sh_rows[...], scaled).astype(bf16)
                for t in range(trans):
                    first = 2 * t * height
                    x_ph[t, s, place, 0:order] = moved[first : first + height]
                    x_ph[t, s, place, order:] = moved[first + height : first + 2 * height]
                if s == 1:
                    moved = dot(fl_rows[...], scaled).astype(bf16)
                    for t in range(trans):
                        first = 2 * t * height
                        x_pp[t, place, 0:order] = moved[first : first + height]
                        x_pp[t, place, order:] = moved[first + height : first + 2 * height]
                else:
                    upper = dot(band[...], scaled).astype(bf16)
                left = lax.dot_general(band[...], scaled, NT, preferred_element_type=f32)
                lefts.append(left.astype(bf16))
            lefts.append(upper)
            joined = jnp.concatenate(
                [jnp.concatenate([one[:height], one[height:]], 1) for one in lefts], 0
            )
            second = dot(joined, col_table[...])
            for part in range(3):
                fixed[part, place, :] = second[part * height : (part + 1) * height]

    @pl.loop(0, reach + 3)
    def _(k):
        @pl.when(jnp.logical_and(k >= 1, k <= reach))
        def _():
            arrival(k, group).wait_recv()
            for step in range(1, chips):
                to_far(k, step).start()
            to_core(k).start()

        @pl.when(jnp.logical_and(k >= 2, k <= reach + 1))
        def _():
            for step in range(1, chips):
                arrival(k - 1, far(step)).wait_recv()
                relay(k - 1, step).start()

        @pl.when(k == 2)
        def _():
            local[0].wait()
            local[1].wait()

        @pl.when(k >= 3)
        def _():
            arrival(k - 2, partner).wait_recv()
            for step in range(1, chips):
                piece = lax.rem(chip + step, chips) * 2 + (1 - core)
                arrival(k - 2, piece).wait_recv()
            direct(k - 2)[1].wait_recv()

        @pl.when(k >= 2)
        def _():
            absorb(k - 2)

    local[2].wait()
    local[3].wait()
    length = (reach + 1) * walkers

    def product(left, right):
        for v in range(length):
            part = slice(v * height, (v + 1) * height)
            a, b = left[part, 0:order], left[part, order:]
            c, d = right[part, 0:order], right[part, order:]
            yield a, b, c, d

    @pl.loop(0, trans)
    def _(t):
        real, imag = ph_out[0, t], ph_out[1, t]
        for s in range(2):
            moved = dot(x_ph[t, s], sh_cols[t])
            for a, b, c, d in product(fixed[s], moved):
                real = real + (a * c + b * d)
                imag = imag + (a * d - b * c)
        ph_out[0, t] = real
        ph_out[1, t] = imag
        real, imag = pp_out[0, t], pp_out[1, t]
        lowered = dot(x_pp[t], fl_cols[t])
        for a, b, c, d in product(fixed[2], lowered):
            real = real + (a * c - b * d)
            imag = imag + (a * d + b * c)
        pp_out[0, t] = real
        pp_out[1, t] = imag

    for offset in range(1, reach + 1):
        for copy in direct(offset):
            copy.wait_send()
        to_core(offset).wait_send()
        for step in range(1, chips):
            to_far(offset, step).wait_send()
            relay(offset, step).wait_send()


def on_device(masses, spins, shift_table, flip_table, ph_in, pp_in):
    groups = lax.axis_size("grp")
    blocks = lax.axis_size("blk")
    reach = min(8, blocks - 1)
    visits = reach + 1
    walkers, _, order, _ = masses.shape
    trans = shift_table.shape[0]
    height = order // groups
    chips = groups // 2
    f32, bf16 = jnp.float32, jnp.bfloat16
    dma = pltpu.SemaphoreType.DMA
    anywhere = pl.BlockSpec(memory_space=pl.ANY)
    return pl.pallas_call(
        functools.partial(kernel, blocks, groups, reach),
        out_shape=(
            jax.ShapeDtypeStruct(ph_in.shape, f32),
            jax.ShapeDtypeStruct(pp_in.shape, f32),
        ),
        in_specs=[pl.BlockSpec(memory_space=pltpu.SMEM)] + [anywhere] * 4,
        out_specs=(pl.BlockSpec(memory_space=pltpu.VMEM),) * 2,
        scratch_shapes=[
            pltpu.VMEM((visits, walkers, 2, order, order), bf16),
            pltpu.VMEM((visits, walkers, order), jnp.int32),
            pltpu.VMEM((2 * order, 2 * order), bf16),
            pltpu.VMEM((trans, 2 * order, 2 * order), bf16),
            pltpu.VMEM((trans, 2 * order, 2 * order), bf16),
            pltpu.VMEM((2 * height, order), bf16),
            pltpu.VMEM((trans * 2 * height, order), bf16),
            pltpu.VMEM((trans * 2 * height, order), bf16),
            pltpu.VMEM((trans, 2, visits * walkers * height, 2 * order), bf16),
            pltpu.VMEM((trans, visits * walkers * height, 2 * order), bf16),
            pltpu.VMEM((3, visits * walkers * height, 2 * order), f32),
            dma((visits, groups)),
            dma((visits,)),
            dma((visits,)),
            dma((visits,)),
            dma((visits,)),
            dma((chips, visits)),
            dma((chips, visits)),
            dma((4,)),
        ],
        compiler_params=pltpu.CompilerParams(
            collective_id=0, has_side_effects=True, vmem_limit_bytes=56 * 1024 * 1024
        ),
    )(shift_table, masses, spins, ph_in, pp_in)


def solution(mesh):
    placed = (
        P("blk", None, None, None),
        P("blk", None),
        P("blk", None),
        P("blk", None),
        P(None, "blk", "grp", None),
        P(None, "blk", "grp", None),
    )
    return jax.shard_map(
        on_device,
        mesh=mesh,
        in_specs=placed,
        out_specs=(P(None, "blk", "grp", None), P(None, "blk", "grp", None)),
        check_vma=False,
    )
```

```python
import functools
import math

import jax
import jax.numpy as jnp
from jax import lax
from jax.experimental import pallas as pl
from jax.experimental.pallas import tpu as pltpu
from jax.sharding import PartitionSpec as P

NW = 16
NK = 16
COUPLING = 0.5
DIRECT = 6
LAG = 2
MESH = pl.DeviceIdType.MESH
NT = (((1,), (1,)), ((), ()))


def angle(steps):
    return steps.astype(jnp.float32) * (math.pi / NW)


def base_steps(row, col):
    return ((2 * (row // NK) + 1) * (col // NK) - 2 * (row % NK) * (col % NK)) % (2 * NW)


def move_steps(freq, mom, col):
    return (2 * freq * (col // NK) - 2 * mom * (col % NK)) % (2 * NW)


def kernel(
    blocks, groups, reach, shift_ref, masses_ref, spins_ref, ph_ref, pp_ref, ph_out, pp_out,
    held, held_spins, col_table, sh_cols, fl_cols, band, sh_rows, fl_rows,
    x_ph, x_pp, fixed, recv_sem, spin_recv, direct_sem, spin_send, core_sem, far_sem, relay_sem,
    local_sem,
):
    group = lax.axis_index("grp")
    block = lax.axis_index("blk")
    order = held.shape[-1]
    walkers = held.shape[1]
    trans = ph_out.shape[1]
    height = order // groups
    chips = groups // 2
    chip, core = group // 2, group % 2
    partner = chip * 2 + (1 - core)
    f32, bf16 = jnp.float32, jnp.bfloat16

    def far(step):
        return lax.rem(chip + step, chips) * 2 + core

    def rows_of(piece):
        return pl.ds(pl.multiple_of(piece * height, height), height)

    gather = reach + 1 == blocks and blocks % 2 == 0 and chips == 2
    layers = blocks // 2
    layer, side = block // 2, block % 2

    def along(offset):
        return lax.rem(layer + offset + layers, layers) * 2 + side

    beside = layer * 2 + (1 - side)
    half = order // 2
    own_rows, far_rows = half * DIRECT // 8, half * (8 - DIRECT) // 8
    own_first = core * half + chip * far_rows
    give_first = core * half + chip * own_rows
    take_first = core * half + (1 - chip) * own_rows
    both_first = core * half + far_rows
    both_rows = own_rows - far_rows
    home = block if gather else 0
    near = [sorted(set(range(layers)) - {one}, key=lambda z: abs(z - one)) for one in range(layers)]

    def near_layer(rank):
        found = 0
        for one in range(layers):
            for i in range(layers - 1):
                hit = jnp.logical_and(layer == one, rank == i)
                found = found + jnp.where(hit, near[one][i], 0)
        return found

    def source_of(step):
        rank = lax.rem(step + layers - 2, layers - 1)
        direct_side = jnp.where(step <= layers, side, 1 - side)
        found = near_layer(rank) * 2 + direct_side
        return jnp.where(step == 0, block, jnp.where(step == 1, beside, found))

    barrier = pltpu.get_barrier_semaphore()
    if gather:
        sources = [along(offset) for offset in range(1, layers)] + [beside]
    else:
        sources = [lax.rem(block - offset + blocks, blocks) for offset in range(1, reach + 1)]
    for source in sources:
        pl.semaphore_signal(barrier, inc=1, device_id=(group, source), device_id_type=MESH)
    pl.semaphore_signal(barrier, inc=1, device_id=(partner, block), device_id_type=MESH)
    for step in range(1, chips):
        pl.semaphore_signal(barrier, inc=1, device_id=(far(step), block), device_id_type=MESH)

    local = [
        pltpu.make_async_copy(masses_ref, held.at[home], local_sem.at[0]),
        pltpu.make_async_copy(spins_ref, held_spins.at[home], local_sem.at[1]),
        pltpu.make_async_copy(ph_ref, ph_out, local_sem.at[2]),
        pltpu.make_async_copy(pp_ref, pp_out, local_sem.at[3]),
    ]
    for copy in local:
        copy.start()
    pl.semaphore_wait(barrier, len(sources) + chips)

    def direct(offset):
        target = (group, lax.rem(block + offset, blocks))
        return (
            pltpu.make_async_remote_copy(
                src_ref=masses_ref.at[:, :, rows_of(group)],
                dst_ref=held.at[offset, :, :, rows_of(group)],
                send_sem=direct_sem.at[offset, 0],
                recv_sem=recv_sem.at[offset, group],
                device_id=target,
                device_id_type=MESH,
            ),
            pltpu.make_async_remote_copy(
                src_ref=spins_ref,
                dst_ref=held_spins.at[offset],
                send_sem=spin_send.at[offset, 0],
                recv_sem=spin_recv.at[offset],
                device_id=target,
                device_id_type=MESH,
            ),
        )

    def passed(offset, piece, target, send_sem):
        view = held.at[offset, :, :, rows_of(piece)]
        return pltpu.make_async_remote_copy(
            src_ref=view,
            dst_ref=view,
            send_sem=send_sem,
            recv_sem=recv_sem.at[offset, piece],
            device_id=(target, block),
            device_id_type=MESH,
        )

    def to_core(offset):
        return passed(offset, group, partner, core_sem.at[offset, 0])

    def to_far(offset, step):
        return passed(offset, group, far(step), far_sem.at[step, offset])

    def relay(offset, step):
        return passed(offset, far(step), partner, relay_sem.at[step, offset])

    def arrival(offset, piece):
        return passed(offset, piece, partner, core_sem.at[offset, 0])

    def send(src, dst, send_sem, recv, target):
        return pltpu.make_async_remote_copy(
            src_ref=src,
            dst_ref=dst,
            send_sem=send_sem,
            recv_sem=recv,
            device_id=target,
            device_id_type=MESH,
        )

    def block_rows(slot, first, count):
        return held.at[slot, :, :, pl.ds(pl.multiple_of(first, 16), count)]

    def part_of(piece):
        return ((give_first, far_rows), (both_first, both_rows))[piece]

    def hop(slot, target, piece, own):
        first, count = part_of(piece)
        dst = block_rows(slot, first, count)
        src = masses_ref.at[:, :, pl.ds(pl.multiple_of(first, 16), count)] if own else dst
        return send(src, dst, direct_sem.at[slot if not own else target, piece + 2 * own],
                    recv_sem.at[slot, piece], (group, target))

    def note(slot, target, own):
        return send(spins_ref if own else held_spins.at[slot], held_spins.at[slot],
                    spin_send.at[slot if not own else target, 0 + own], spin_recv.at[slot],
                    (group, target))

    def own_hops():
        targets = [beside] + [near_layer(i) * 2 + side for i in range(layers - 1)]
        return [hop(block, target, 0, 1) for target in targets] + [
            copy for target in targets
            for copy in (note(block, target, 1), hop(block, target, 1, 1))
        ]

    def across(slot):
        view = block_rows(slot, give_first, far_rows)
        return send(view, view, far_sem.at[0, slot], recv_sem.at[slot, 2], (far(1), block))

    def taken(slot):
        view = block_rows(slot, take_first, far_rows)
        return send(view, view, far_sem.at[0, slot], recv_sem.at[slot, 2], (far(1), block))

    def share(slot):
        view = block_rows(slot, own_first, own_rows)
        return send(view, view, core_sem.at[slot, 0], recv_sem.at[slot, 3], (partner, block))

    def share_taken(slot):
        view = block_rows(slot, take_first, far_rows)
        return send(view, view, core_sem.at[slot, 1], recv_sem.at[slot, 4], (partner, block))

    if gather:
        for copy in own_hops():
            copy.start()
    else:
        for offset in range(1, reach + 1):
            for copy in direct(offset):
                copy.start()

    norm = 1.0 / math.sqrt(NW * NK)
    index_col = lax.broadcasted_iota(jnp.int32, (order, 128), 0)
    lane = lax.broadcasted_iota(jnp.int32, (order, 128), 1)
    freq = jnp.zeros((order, 128), jnp.int32)
    mom = jnp.zeros((order, 128), jnp.int32)
    for t in range(trans):
        start = shift_ref[t, 0]
        freq = jnp.where(lane == t, start // NK, freq)
        mom = jnp.where(lane == t, start % NK, mom)
    move = angle(move_steps(freq, mom, index_col))
    move_cos, move_sin = jnp.cos(move), jnp.sin(move)

    def put_cols(ref, t, real, imag):
        where = (slice(None),) if t is None else (t, slice(None))
        real, imag = (real * norm).astype(bf16), (imag * norm).astype(bf16)
        ref[where[:-1] + (slice(0, order), slice(0, order))] = real
        ref[where[:-1] + (slice(0, order), slice(order, 2 * order))] = -imag
        ref[where[:-1] + (slice(order, 2 * order), slice(0, order))] = imag
        ref[where[:-1] + (slice(order, 2 * order), slice(order, 2 * order))] = real

    site = lax.broadcasted_iota(jnp.int32, (order, order), 0)
    momentum = lax.broadcasted_iota(jnp.int32, (order, order), 1)
    phase = angle(base_steps(momentum, site))
    cos, sin = jnp.cos(phase), jnp.sin(phase)
    put_cols(col_table, None, cos, sin)
    for t in range(trans):
        mc, ms = move_cos[:, t : t + 1], move_sin[:, t : t + 1]
        cc, ss, sc, cs = mc * cos, ms * sin, ms * cos, mc * sin
        put_cols(sh_cols, t, cc - ss, sc + cs)
        put_cols(fl_cols, t, cc + ss, sc - cs)

    row = lax.broadcasted_iota(jnp.int32, (height, order), 0) + group * height
    column = lax.broadcasted_iota(jnp.int32, (height, order), 1)
    phase = angle(base_steps(row, column))
    cos, sin = jnp.cos(phase), jnp.sin(phase)
    band[0:height, :] = (cos * norm).astype(bf16)
    band[height : 2 * height, :] = (sin * norm).astype(bf16)
    col8 = lax.broadcasted_iota(jnp.int32, (8, order), 1)
    for t in range(trans):
        start = shift_ref[t, 0]
        move = angle(move_steps(start // NK, start % NK, col8))
        mc, ms = jnp.cos(move)[0:1], jnp.sin(move)[0:1]
        cc, ss, sc, cs = mc * cos, ms * sin, ms * cos, mc * sin
        first = 2 * t * height
        sh_rows[first : first + height, :] = ((cc - ss) * norm).astype(bf16)
        sh_rows[first + height : first + 2 * height, :] = ((sc + cs) * norm).astype(bf16)
        fl_rows[first : first + height, :] = ((cc + ss) * norm).astype(bf16)
        fl_rows[first + height : first + 2 * height, :] = ((sc - cs) * norm).astype(bf16)

    def dot(a, b):
        return jnp.dot(a, b, preferred_element_type=f32)

    def absorb(slot):
        for w in range(walkers):
            place = pl.ds(pl.multiple_of((slot * walkers + w) * height, height), height)
            signed = (2 * held_spins[slot, w : w + 1, :] - 1).astype(f32)
            lefts = []
            for s in range(2):
                factor = jnp.exp((COUPLING if s == 0 else -COUPLING) * signed)
                scaled = (held[slot, w, s].astype(f32) * factor).astype(bf16)
                moved = dot(sh_rows[...], scaled).astype(bf16)
                for t in range(trans):
                    first = 2 * t * height
                    x_ph[t, s, place, 0:order] = moved[first : first + height]
                    x_ph[t, s, place, order:] = moved[first + height : first + 2 * height]
                if s == 1:
                    moved = dot(fl_rows[...], scaled).astype(bf16)
                    for t in range(trans):
                        first = 2 * t * height
                        x_pp[t, place, 0:order] = moved[first : first + height]
                        x_pp[t, place, order:] = moved[first + height : first + 2 * height]
                else:
                    upper = dot(band[...], scaled).astype(bf16)
                left = lax.dot_general(band[...], scaled, NT, preferred_element_type=f32)
                lefts.append(left.astype(bf16))
            lefts.append(upper)
            joined = jnp.concatenate(
                [jnp.concatenate([one[:height], one[height:]], 1) for one in lefts], 0
            )
            second = dot(joined, col_table[...])
            for part in range(3):
                fixed[part, place, :] = second[part * height : (part + 1) * height]

    if gather:

        @pl.loop(0, reach + LAG + 2)
        def _(k):
            @pl.when(jnp.logical_and(k >= 1, k <= reach))
            def _():
                slot = source_of(k)
                hop(slot, beside, 0, 0).wait_recv()
                across(slot).start()

                @pl.when(jnp.logical_and(k >= 2, k <= layers))
                def _():
                    hop(slot, beside, 0, 0).start()

            @pl.when(jnp.logical_and(k >= LAG + 1, k <= reach + LAG))
            def _():
                slot = source_of(k - LAG)
                hop(slot, beside, 1, 0).wait_recv()
                note(slot, beside, 0).wait_recv()

                @pl.when(jnp.logical_and(k >= LAG + 2, k <= layers + LAG))
                def _():
                    hop(slot, beside, 1, 0).start()
                    note(slot, beside, 0).start()

                share(slot).start()
                taken(slot).wait_recv()
                share_taken(slot).start()

            @pl.when(k == LAG + 1)
            def _():
                local[0].wait()
                local[1].wait()

            @pl.when(k >= LAG + 2)
            def _():
                slot = source_of(k - LAG - 1)
                share(slot).wait_recv()
                share_taken(slot).wait_recv()

            @pl.when(k >= LAG + 1)
            def _():
                absorb(source_of(k - LAG - 1))

    else:

        @pl.loop(0, reach + 3)
        def _(k):
            @pl.when(jnp.logical_and(k >= 1, k <= reach))
            def _():
                arrival(k, group).wait_recv()
                for step in range(1, chips):
                    to_far(k, step).start()
                to_core(k).start()

            @pl.when(jnp.logical_and(k >= 2, k <= reach + 1))
            def _():
                for step in range(1, chips):
                    arrival(k - 1, far(step)).wait_recv()
                    relay(k - 1, step).start()

            @pl.when(k == 2)
            def _():
                local[0].wait()
                local[1].wait()

            @pl.when(k >= 3)
            def _():
                arrival(k - 2, partner).wait_recv()
                for step in range(1, chips):
                    piece = lax.rem(chip + step, chips) * 2 + (1 - core)
                    arrival(k - 2, piece).wait_recv()
                direct(k - 2)[1].wait_recv()

            @pl.when(k >= 2)
            def _():
                absorb(k - 2)

    local[2].wait()
    local[3].wait()
    length = (reach + 1) * walkers

    def product(left, right):
        for v in range(length):
            part = slice(v * height, (v + 1) * height)
            a, b = left[part, 0:order], left[part, order:]
            c, d = right[part, 0:order], right[part, order:]
            yield a, b, c, d

    @pl.loop(0, trans)
    def _(t):
        real, imag = ph_out[0, t], ph_out[1, t]
        for s in range(2):
            moved = dot(x_ph[t, s], sh_cols[t])
            for a, b, c, d in product(fixed[s], moved):
                real = real + (a * c + b * d)
                imag = imag + (a * d - b * c)
        ph_out[0, t] = real
        ph_out[1, t] = imag
        real, imag = pp_out[0, t], pp_out[1, t]
        lowered = dot(x_pp[t], fl_cols[t])
        for a, b, c, d in product(fixed[2], lowered):
            real = real + (a * c - b * d)
            imag = imag + (a * d + b * c)
        pp_out[0, t] = real
        pp_out[1, t] = imag

    if gather:
        for copy in own_hops():
            copy.wait_send()
        for step in range(1, reach + 1):
            slot = source_of(step)
            if 2 <= step <= layers:
                hop(slot, beside, 0, 0).wait_send()
                hop(slot, beside, 1, 0).wait_send()
                note(slot, beside, 0).wait_send()
            across(slot).wait_send()
            share(slot).wait_send()
            share_taken(slot).wait_send()
    else:
        for offset in range(1, reach + 1):
            for copy in direct(offset):
                copy.wait_send()
            to_core(offset).wait_send()
            for step in range(1, chips):
                to_far(offset, step).wait_send()
                relay(offset, step).wait_send()


def on_device(masses, spins, shift_table, flip_table, ph_in, pp_in):
    groups = lax.axis_size("grp")
    blocks = lax.axis_size("blk")
    reach = min(8, blocks - 1)
    visits = reach + 1
    walkers, _, order, _ = masses.shape
    trans = shift_table.shape[0]
    height = order // groups
    chips = groups // 2
    f32, bf16 = jnp.float32, jnp.bfloat16
    dma = pltpu.SemaphoreType.DMA
    anywhere = pl.BlockSpec(memory_space=pl.ANY)
    return pl.pallas_call(
        functools.partial(kernel, blocks, groups, reach),
        out_shape=(
            jax.ShapeDtypeStruct(ph_in.shape, f32),
            jax.ShapeDtypeStruct(pp_in.shape, f32),
        ),
        in_specs=[pl.BlockSpec(memory_space=pltpu.SMEM)] + [anywhere] * 4,
        out_specs=(pl.BlockSpec(memory_space=pltpu.VMEM),) * 2,
        scratch_shapes=[
            pltpu.VMEM((visits, walkers, 2, order, order), bf16),
            pltpu.VMEM((visits, walkers, order), jnp.int32),
            pltpu.VMEM((2 * order, 2 * order), bf16),
            pltpu.VMEM((trans, 2 * order, 2 * order), bf16),
            pltpu.VMEM((trans, 2 * order, 2 * order), bf16),
            pltpu.VMEM((2 * height, order), bf16),
            pltpu.VMEM((trans * 2 * height, order), bf16),
            pltpu.VMEM((trans * 2 * height, order), bf16),
            pltpu.VMEM((trans, 2, visits * walkers * height, 2 * order), bf16),
            pltpu.VMEM((trans, visits * walkers * height, 2 * order), bf16),
            pltpu.VMEM((3, visits * walkers * height, 2 * order), f32),
            dma((visits, max(groups, 5))),
            dma((visits,)),
            dma((visits, 4)),
            dma((visits, 2)),
            dma((visits, 2)),
            dma((chips, visits)),
            dma((chips, visits)),
            dma((4,)),
        ],
        compiler_params=pltpu.CompilerParams(
            collective_id=0, has_side_effects=True, vmem_limit_bytes=56 * 1024 * 1024
        ),
    )(shift_table, masses, spins, ph_in, pp_in)


def solution(mesh):
    placed = (
        P("blk", None, None, None),
        P("blk", None),
        P("blk", None),
        P("blk", None),
        P(None, "blk", "grp", None),
        P(None, "blk", "grp", None),
    )
    return jax.shard_map(
        on_device,
        mesh=mesh,
        in_specs=placed,
        out_specs=(P(None, "blk", "grp", None), P(None, "blk", "grp", None)),
        check_vma=False,
    )
```

```python
import functools
import math

import jax
import jax.numpy as jnp
from jax import lax
from jax.experimental import pallas as pl
from jax.experimental.pallas import tpu as pltpu
from jax.sharding import PartitionSpec as P

NW = 16
NK = 16
COUPLING = 0.5
DIRECT = 6
LAG = 2
MESH = pl.DeviceIdType.MESH
NT = (((1,), (1,)), ((), ()))


def angle(steps):
    return steps.astype(jnp.float32) * (math.pi / NW)


def base_steps(row, col):
    return ((2 * (row // NK) + 1) * (col // NK) - 2 * (row % NK) * (col % NK)) % (2 * NW)


def move_steps(freq, mom, col):
    return (2 * freq * (col // NK) - 2 * mom * (col % NK)) % (2 * NW)


def kernel(
    blocks, groups, reach, shift_ref, masses_ref, spins_ref, ph_ref, pp_ref, ph_out, pp_out,
    held, held_spins, col_table, sh_cols, fl_cols, band, sh_rows, fl_rows,
    x_ph, x_pp, fixed, recv_sem, spin_recv, direct_sem, spin_send, core_sem, far_sem, relay_sem,
    local_sem,
):
    group = lax.axis_index("grp")
    block = lax.axis_index("blk")
    order = held.shape[-1]
    walkers = held.shape[1]
    trans = ph_out.shape[1]
    height = order // groups
    chips = groups // 2
    chip, core = group // 2, group % 2
    partner = chip * 2 + (1 - core)
    f32, bf16 = jnp.float32, jnp.bfloat16

    def far(step):
        return lax.rem(chip + step, chips) * 2 + core

    def rows_of(piece):
        return pl.ds(pl.multiple_of(piece * height, height), height)

    gather = reach + 1 == blocks and blocks % 2 == 0 and chips == 2
    layers = blocks // 2
    layer, side = block // 2, block % 2

    def along(offset):
        return lax.rem(layer + offset + layers, layers) * 2 + side

    beside = layer * 2 + (1 - side)
    half = order // 2
    own_rows, far_rows = half * DIRECT // 8, half * (8 - DIRECT) // 8
    own_first = core * half + chip * far_rows
    give_first = core * half + chip * own_rows
    take_first = core * half + (1 - chip) * own_rows
    both_first = core * half + far_rows
    both_rows = own_rows - far_rows
    home = block if gather else 0
    near = [sorted(set(range(layers)) - {one}, key=lambda z: abs(z - one)) for one in range(layers)]

    def near_layer(rank):
        found = 0
        for one in range(layers):
            for i in range(layers - 1):
                hit = jnp.logical_and(layer == one, rank == i)
                found = found + jnp.where(hit, near[one][i], 0)
        return found

    def source_of(step):
        rank = lax.rem(step + 2 * layers - 4, layers - 1)
        direct_side = jnp.where(step <= layers, side, 1 - side)
        found = near_layer(rank) * 2 + direct_side
        return jnp.where(step == 0, block, jnp.where(step == 1, beside, found))

    barrier = pltpu.get_barrier_semaphore()
    if gather:
        sources = [along(offset) for offset in range(1, layers)] + [beside]
    else:
        sources = [lax.rem(block - offset + blocks, blocks) for offset in range(1, reach + 1)]
    for source in sources:
        pl.semaphore_signal(barrier, inc=1, device_id=(group, source), device_id_type=MESH)
    pl.semaphore_signal(barrier, inc=1, device_id=(partner, block), device_id_type=MESH)
    for step in range(1, chips):
        pl.semaphore_signal(barrier, inc=1, device_id=(far(step), block), device_id_type=MESH)

    local = [
        pltpu.make_async_copy(masses_ref, held.at[home], local_sem.at[0]),
        pltpu.make_async_copy(spins_ref, held_spins.at[home], local_sem.at[1]),
        pltpu.make_async_copy(ph_ref, ph_out, local_sem.at[2]),
        pltpu.make_async_copy(pp_ref, pp_out, local_sem.at[3]),
    ]
    for copy in local:
        copy.start()
    pl.semaphore_wait(barrier, len(sources) + chips)

    def direct(offset):
        target = (group, lax.rem(block + offset, blocks))
        return (
            pltpu.make_async_remote_copy(
                src_ref=masses_ref.at[:, :, rows_of(group)],
                dst_ref=held.at[offset, :, :, rows_of(group)],
                send_sem=direct_sem.at[offset, 0],
                recv_sem=recv_sem.at[offset, group],
                device_id=target,
                device_id_type=MESH,
            ),
            pltpu.make_async_remote_copy(
                src_ref=spins_ref,
                dst_ref=held_spins.at[offset],
                send_sem=spin_send.at[offset, 0],
                recv_sem=spin_recv.at[offset],
                device_id=target,
                device_id_type=MESH,
            ),
        )

    def passed(offset, piece, target, send_sem):
        view = held.at[offset, :, :, rows_of(piece)]
        return pltpu.make_async_remote_copy(
            src_ref=view,
            dst_ref=view,
            send_sem=send_sem,
            recv_sem=recv_sem.at[offset, piece],
            device_id=(target, block),
            device_id_type=MESH,
        )

    def to_core(offset):
        return passed(offset, group, partner, core_sem.at[offset, 0])

    def to_far(offset, step):
        return passed(offset, group, far(step), far_sem.at[step, offset])

    def relay(offset, step):
        return passed(offset, far(step), partner, relay_sem.at[step, offset])

    def arrival(offset, piece):
        return passed(offset, piece, partner, core_sem.at[offset, 0])

    def send(src, dst, send_sem, recv, target):
        return pltpu.make_async_remote_copy(
            src_ref=src,
            dst_ref=dst,
            send_sem=send_sem,
            recv_sem=recv,
            device_id=target,
            device_id_type=MESH,
        )

    def block_rows(slot, first, count):
        return held.at[slot, :, :, pl.ds(pl.multiple_of(first, 16), count)]

    def part_of(piece):
        return ((give_first, far_rows), (both_first, both_rows))[piece]

    def hop(slot, target, piece, own):
        first, count = part_of(piece)
        dst = block_rows(slot, first, count)
        src = masses_ref.at[:, :, pl.ds(pl.multiple_of(first, 16), count)] if own else dst
        return send(src, dst, direct_sem.at[slot if not own else target, piece + 2 * own],
                    recv_sem.at[slot, piece], (group, target))

    def note(slot, target, own):
        return send(spins_ref if own else held_spins.at[slot], held_spins.at[slot],
                    spin_send.at[slot if not own else target, 0 + own], spin_recv.at[slot],
                    (group, target))

    def own_hops():
        targets = [beside] + [near_layer(i) * 2 + side for i in range(layers - 1)]
        return [hop(block, target, 0, 1) for target in targets] + [
            copy for target in targets
            for copy in (note(block, target, 1), hop(block, target, 1, 1))
        ]

    def across(slot):
        view = block_rows(slot, give_first, far_rows)
        return send(view, view, far_sem.at[0, slot], recv_sem.at[slot, 2], (far(1), block))

    def taken(slot):
        view = block_rows(slot, take_first, far_rows)
        return send(view, view, far_sem.at[0, slot], recv_sem.at[slot, 2], (far(1), block))

    def share(slot):
        view = block_rows(slot, own_first, own_rows)
        return send(view, view, core_sem.at[slot, 0], recv_sem.at[slot, 3], (partner, block))

    def share_taken(slot):
        view = block_rows(slot, take_first, far_rows)
        return send(view, view, core_sem.at[slot, 1], recv_sem.at[slot, 4], (partner, block))

    if gather:
        for copy in own_hops():
            copy.start()
    else:
        for offset in range(1, reach + 1):
            for copy in direct(offset):
                copy.start()

    norm = 1.0 / math.sqrt(NW * NK)
    index_col = lax.broadcasted_iota(jnp.int32, (order, 128), 0)
    lane = lax.broadcasted_iota(jnp.int32, (order, 128), 1)
    freq = jnp.zeros((order, 128), jnp.int32)
    mom = jnp.zeros((order, 128), jnp.int32)
    for t in range(trans):
        start = shift_ref[t, 0]
        freq = jnp.where(lane == t, start // NK, freq)
        mom = jnp.where(lane == t, start % NK, mom)
    move = angle(move_steps(freq, mom, index_col))
    move_cos, move_sin = jnp.cos(move), jnp.sin(move)

    def put_cols(ref, t, real, imag):
        where = (slice(None),) if t is None else (t, slice(None))
        real, imag = (real * norm).astype(bf16), (imag * norm).astype(bf16)
        ref[where[:-1] + (slice(0, order), slice(0, order))] = real
        ref[where[:-1] + (slice(0, order), slice(order, 2 * order))] = -imag
        ref[where[:-1] + (slice(order, 2 * order), slice(0, order))] = imag
        ref[where[:-1] + (slice(order, 2 * order), slice(order, 2 * order))] = real

    site = lax.broadcasted_iota(jnp.int32, (order, order), 0)
    momentum = lax.broadcasted_iota(jnp.int32, (order, order), 1)
    phase = angle(base_steps(momentum, site))
    cos, sin = jnp.cos(phase), jnp.sin(phase)
    put_cols(col_table, None, cos, sin)
    for t in range(trans):
        mc, ms = move_cos[:, t : t + 1], move_sin[:, t : t + 1]
        cc, ss, sc, cs = mc * cos, ms * sin, ms * cos, mc * sin
        put_cols(sh_cols, t, cc - ss, sc + cs)
        put_cols(fl_cols, t, cc + ss, sc - cs)

    row = lax.broadcasted_iota(jnp.int32, (height, order), 0) + group * height
    column = lax.broadcasted_iota(jnp.int32, (height, order), 1)
    phase = angle(base_steps(row, column))
    cos, sin = jnp.cos(phase), jnp.sin(phase)
    band[0:height, :] = (cos * norm).astype(bf16)
    band[height : 2 * height, :] = (sin * norm).astype(bf16)
    col8 = lax.broadcasted_iota(jnp.int32, (8, order), 1)
    for t in range(trans):
        start = shift_ref[t, 0]
        move = angle(move_steps(start // NK, start % NK, col8))
        mc, ms = jnp.cos(move)[0:1], jnp.sin(move)[0:1]
        cc, ss, sc, cs = mc * cos, ms * sin, ms * cos, mc * sin
        first = 2 * t * height
        sh_rows[first : first + height, :] = ((cc - ss) * norm).astype(bf16)
        sh_rows[first + height : first + 2 * height, :] = ((sc + cs) * norm).astype(bf16)
        fl_rows[first : first + height, :] = ((cc + ss) * norm).astype(bf16)
        fl_rows[first + height : first + 2 * height, :] = ((sc - cs) * norm).astype(bf16)

    def dot(a, b):
        return jnp.dot(a, b, preferred_element_type=f32)

    def absorb(slot):
        for w in range(walkers):
            place = pl.ds(pl.multiple_of((slot * walkers + w) * height, height), height)
            signed = (2 * held_spins[slot, w : w + 1, :] - 1).astype(f32)
            lefts = []
            for s in range(2):
                factor = jnp.exp((COUPLING if s == 0 else -COUPLING) * signed)
                scaled = (held[slot, w, s].astype(f32) * factor).astype(bf16)
                moved = dot(sh_rows[...], scaled).astype(bf16)
                for t in range(trans):
                    first = 2 * t * height
                    x_ph[t, s, place, 0:order] = moved[first : first + height]
                    x_ph[t, s, place, order:] = moved[first + height : first + 2 * height]
                if s == 1:
                    moved = dot(fl_rows[...], scaled).astype(bf16)
                    for t in range(trans):
                        first = 2 * t * height
                        x_pp[t, place, 0:order] = moved[first : first + height]
                        x_pp[t, place, order:] = moved[first + height : first + 2 * height]
                else:
                    upper = dot(band[...], scaled).astype(bf16)
                left = lax.dot_general(band[...], scaled, NT, preferred_element_type=f32)
                lefts.append(left.astype(bf16))
            lefts.append(upper)
            joined = jnp.concatenate(
                [jnp.concatenate([one[:height], one[height:]], 1) for one in lefts], 0
            )
            second = dot(joined, col_table[...])
            for part in range(3):
                fixed[part, place, :] = second[part * height : (part + 1) * height]

    if gather:

        @pl.loop(0, reach + LAG + 2)
        def _(k):
            @pl.when(jnp.logical_and(k >= 1, k <= reach))
            def _():
                slot = source_of(k)
                hop(slot, beside, 0, 0).wait_recv()
                across(slot).start()

                @pl.when(jnp.logical_and(k >= 2, k <= layers))
                def _():
                    hop(slot, beside, 0, 0).start()

            @pl.when(jnp.logical_and(k >= LAG + 1, k <= reach + LAG))
            def _():
                slot = source_of(k - LAG)
                hop(slot, beside, 1, 0).wait_recv()
                note(slot, beside, 0).wait_recv()

                @pl.when(jnp.logical_and(k >= LAG + 2, k <= layers + LAG))
                def _():
                    hop(slot, beside, 1, 0).start()
                    note(slot, beside, 0).start()

                share(slot).start()
                taken(slot).wait_recv()
                share_taken(slot).start()

            @pl.when(k == LAG + 1)
            def _():
                local[0].wait()
                local[1].wait()

            @pl.when(k >= LAG + 2)
            def _():
                slot = source_of(k - LAG - 1)
                share(slot).wait_recv()
                share_taken(slot).wait_recv()

            @pl.when(k >= LAG + 1)
            def _():
                absorb(source_of(k - LAG - 1))

    else:

        @pl.loop(0, reach + 3)
        def _(k):
            @pl.when(jnp.logical_and(k >= 1, k <= reach))
            def _():
                arrival(k, group).wait_recv()
                for step in range(1, chips):
                    to_far(k, step).start()
                to_core(k).start()

            @pl.when(jnp.logical_and(k >= 2, k <= reach + 1))
            def _():
                for step in range(1, chips):
                    arrival(k - 1, far(step)).wait_recv()
                    relay(k - 1, step).start()

            @pl.when(k == 2)
            def _():
                local[0].wait()
                local[1].wait()

            @pl.when(k >= 3)
            def _():
                arrival(k - 2, partner).wait_recv()
                for step in range(1, chips):
                    piece = lax.rem(chip + step, chips) * 2 + (1 - core)
                    arrival(k - 2, piece).wait_recv()
                direct(k - 2)[1].wait_recv()

            @pl.when(k >= 2)
            def _():
                absorb(k - 2)

    local[2].wait()
    local[3].wait()
    length = (reach + 1) * walkers

    def product(left, right):
        for v in range(length):
            part = slice(v * height, (v + 1) * height)
            a, b = left[part, 0:order], left[part, order:]
            c, d = right[part, 0:order], right[part, order:]
            yield a, b, c, d

    @pl.loop(0, trans)
    def _(t):
        real, imag = ph_out[0, t], ph_out[1, t]
        for s in range(2):
            moved = dot(x_ph[t, s], sh_cols[t])
            for a, b, c, d in product(fixed[s], moved):
                real = real + (a * c + b * d)
                imag = imag + (a * d - b * c)
        ph_out[0, t] = real
        ph_out[1, t] = imag
        real, imag = pp_out[0, t], pp_out[1, t]
        lowered = dot(x_pp[t], fl_cols[t])
        for a, b, c, d in product(fixed[2], lowered):
            real = real + (a * c - b * d)
            imag = imag + (a * d + b * c)
        pp_out[0, t] = real
        pp_out[1, t] = imag

    if gather:
        for copy in own_hops():
            copy.wait_send()
        for step in range(1, reach + 1):
            slot = source_of(step)
            if 2 <= step <= layers:
                hop(slot, beside, 0, 0).wait_send()
                hop(slot, beside, 1, 0).wait_send()
                note(slot, beside, 0).wait_send()
            across(slot).wait_send()
            share(slot).wait_send()
            share_taken(slot).wait_send()
    else:
        for offset in range(1, reach + 1):
            for copy in direct(offset):
                copy.wait_send()
            to_core(offset).wait_send()
            for step in range(1, chips):
                to_far(offset, step).wait_send()
                relay(offset, step).wait_send()


def on_device(masses, spins, shift_table, flip_table, ph_in, pp_in):
    groups = lax.axis_size("grp")
    blocks = lax.axis_size("blk")
    reach = min(8, blocks - 1)
    visits = reach + 1
    walkers, _, order, _ = masses.shape
    trans = shift_table.shape[0]
    height = order // groups
    chips = groups // 2
    f32, bf16 = jnp.float32, jnp.bfloat16
    dma = pltpu.SemaphoreType.DMA
    anywhere = pl.BlockSpec(memory_space=pl.ANY)
    return pl.pallas_call(
        functools.partial(kernel, blocks, groups, reach),
        out_shape=(
            jax.ShapeDtypeStruct(ph_in.shape, f32),
            jax.ShapeDtypeStruct(pp_in.shape, f32),
        ),
        in_specs=[pl.BlockSpec(memory_space=pltpu.SMEM)] + [anywhere] * 4,
        out_specs=(pl.BlockSpec(memory_space=pltpu.VMEM),) * 2,
        scratch_shapes=[
            pltpu.VMEM((visits, walkers, 2, order, order), bf16),
            pltpu.VMEM((visits, walkers, order), jnp.int32),
            pltpu.VMEM((2 * order, 2 * order), bf16),
            pltpu.VMEM((trans, 2 * order, 2 * order), bf16),
            pltpu.VMEM((trans, 2 * order, 2 * order), bf16),
            pltpu.VMEM((2 * height, order), bf16),
            pltpu.VMEM((trans * 2 * height, order), bf16),
            pltpu.VMEM((trans * 2 * height, order), bf16),
            pltpu.VMEM((trans, 2, visits * walkers * height, 2 * order), bf16),
            pltpu.VMEM((trans, visits * walkers * height, 2 * order), bf16),
            pltpu.VMEM((3, visits * walkers * height, 2 * order), f32),
            dma((visits, max(groups, 5))),
            dma((visits,)),
            dma((visits, 4)),
            dma((visits, 2)),
            dma((visits, 2)),
            dma((chips, visits)),
            dma((chips, visits)),
            dma((4,)),
        ],
        compiler_params=pltpu.CompilerParams(
            collective_id=0, has_side_effects=True, vmem_limit_bytes=56 * 1024 * 1024
        ),
    )(shift_table, masses, spins, ph_in, pp_in)


def solution(mesh):
    placed = (
        P("blk", None, None, None),
        P("blk", None),
        P("blk", None),
        P("blk", None),
        P(None, "blk", "grp", None),
        P(None, "blk", "grp", None),
    )
    return jax.shard_map(
        on_device,
        mesh=mesh,
        in_specs=placed,
        out_specs=(P(None, "blk", "grp", None), P(None, "blk", "grp", None)),
        check_vma=False,
    )
```
